1024 devices in a mesh: wide: 32 (over z, x_hi), mid: 16 (over y, core), low: 2 (over x_lo).
Axes of the slice: x: 8 (x_hi: 4, x_lo: 2; x = x_hi * 2 + x_lo), y: 8, z: 8, core: 2. Of those that a mesh axis runs over, the one named last changes fastest.
Arguments:
- state: float32 [2, 32, 16, 2, 16384], P(None, 'wide', 'mid', 'low'), may hold values from -6 to 6
- gates: float32 [10, 2, 128, 128], replicated, may hold values from -0.375 to 0.375
- phase_low: float32 [128], replicated, may hold values from -3.140625 to 3.140625
- phase_mid: float32 [128], replicated, may hold values from -3.140625 to 3.140625
- phase_top: float32 [32, 16, 2, 1], P('wide', 'mid', 'low'), may hold values from -3.140625 to 3.140625
- swap_qubits: int32 [2], replicated, may hold values from 0 to 2, as said below
- regroup_order: int32 [4], replicated, may hold values from 0 to 3, each once
Outputs:
- final_state: float32 [2, 32, 16, 2, 16384], P(None, 'wide', 'mid', 'low')
The draws below stay inside these ranges and needn't reach their ends.
Inputs may be any that keep to these rules, and one draw needn't show every extreme that they name: `swap_qubits`: the two entries differ, and one of them is 2. `regroup_order`: each of 0 to 3 once.
All inputs are finite; a program needn't handle non-finite values.
Results may differ from the reference program's by a relative error of at most 0.0003.
Values sent between devices are 32-bit elements; how exact they have to be, the bound alone decides.
A program may use at most 32 MiB of HBM per device.

```python
from functools import partial
import jax
import jax.numpy as jnp
from jax import lax

NG = 10
LQ = 14
WQ = 5
GATE = 128
UPPER = 1
LOCAL = 16384
N_WIDE = 32
N_MID = 16
N_LOW = 2


def draw_swap_qubits(key, part):
    folded = jax.random.fold_in(key, 11)
    first_key, second_key = jax.random.split(folded)
    where_two = jax.random.randint(first_key, (), 0, 2, dtype=jnp.int32)
    other_value = jax.random.randint(second_key, (), 0, 2, dtype=jnp.int32)
    places = jnp.arange(2, dtype=jnp.int32)
    return jnp.where(places == where_two, jnp.int32(2), other_value).astype(jnp.int32)


def block_levels(stream_key, dims, cuts, smallest, top_value):
    def one(position, blocks):
        steps = jax.random.uniform(jax.random.fold_in(jax.random.fold_in(stream_key, 6), position), (blocks,), jnp.float32, smallest / len(cuts), top_value / len(cuts))
        return jnp.repeat(jnp.exp(steps), dims[position] // blocks).reshape((-1,) + (1,) * (len(dims) - position - 1))

    level = one(*cuts[0])
    for cut in cuts[1:]:
        level = level * one(*cut)
    return level


def gaussian(key, extent, width, bound, cuts=(), kind=jnp.bfloat16):
    values = width * jax.random.normal(key, extent, jnp.float32)
    if cuts:
        values = values * block_levels(key, extent, cuts, -0.22, 0.18)
    return jnp.clip(values, -bound, bound).astype(kind)


def setup_inputs(seed: int = 0) -> dict:
    streams_of = jax.random.split(jax.random.key(seed), 8)
    state = gaussian(streams_of[0], (2, N_WIDE, N_MID, N_LOW, LOCAL), 1.0, 6.0, ((1, 32), (2, 16), (3, 2)), jnp.float32)
    gates = gaussian(streams_of[1], (NG, 2, GATE, GATE), (2 * GATE) ** -0.5, 0.375, (), jnp.float32)
    phase_low = jnp.clip(jax.random.uniform(streams_of[2], (GATE,), jnp.float32, -3.140625, 3.140625), -3.140625, 3.140625)
    phase_mid = jnp.clip(jax.random.uniform(streams_of[3], (GATE,), jnp.float32, -3.140625, 3.140625), -3.140625, 3.140625)
    phase_top = jnp.clip(jax.random.uniform(streams_of[4], (N_WIDE, N_MID, N_LOW, UPPER), jnp.float32, -3.140625, 3.140625), -3.140625, 3.140625)
    swap_qubits = draw_swap_qubits(jax.random.fold_in(streams_of[7], 71), 0)
    regroup_order = jax.random.permutation(streams_of[6], 4).astype(jnp.int32)
    return dict(state=state, gates=gates, phase_low=phase_low, phase_mid=phase_mid, phase_top=phase_top, swap_qubits=swap_qubits, regroup_order=regroup_order)


HIGH = lax.Precision.HIGHEST


def gate_inner(vector, real_gate, imag_gate):
    def product(values, matrix):
        return jnp.einsum('...b,ab->...a', values, matrix, precision=HIGH)
    real_part, imag_part = vector[0], vector[1]
    return jnp.stack([product(real_part, real_gate) - product(imag_part, imag_gate),
                      product(real_part, imag_gate) + product(imag_part, real_gate)])


def gate_outer(vector, real_gate, imag_gate):
    def product(values, matrix):
        return jnp.einsum('ab,rbc->rac', matrix, values, precision=HIGH)
    real_part, imag_part = vector[0], vector[1]
    return jnp.stack([product(real_part, real_gate) - product(imag_part, imag_gate),
                      product(real_part, imag_gate) + product(imag_part, real_gate)])


def apply_gate(vector, gates, number):
    if number % 2 == 0:
        result = gate_inner(vector.reshape(2, -1, GATE), gates[number, 0], gates[number, 1])
    else:
        result = gate_outer(vector.reshape(2, -1, GATE, GATE), gates[number, 0], gates[number, 1])
    return result.reshape(2, -1)


def pair_swap(vector, outer_count, inner_count, qubit):
    shaped = vector.reshape(2, outer_count, 2, inner_count, LOCAL >> (qubit + 1), 2, 2 ** qubit)
    shaped = jnp.swapaxes(shaped, 2, 5)
    return shaped.reshape(vector.shape)


def reference(state, gates, phase_low, phase_mid, phase_top, swap_qubits, regroup_order):
    device_count = N_WIDE * N_MID * N_LOW
    vector = apply_gate(state.reshape(2, -1), gates, 0)
    vector = vector.reshape(2, device_count, UPPER, GATE, GATE)
    angle = (phase_top.reshape(device_count, UPPER)[:, :, None, None]
             + phase_mid[None, None, :, None] + phase_low[None, None, None, :])
    cosine = jnp.cos(angle)
    sine_part = jnp.sin(angle)
    vector = jnp.stack([vector[0] * cosine - vector[1] * sine_part,
                        vector[0] * sine_part + vector[1] * cosine]).reshape(2, -1)
    for number in range(1, 4):
        vector = apply_gate(vector, gates, number)
    vector = vector.reshape(2, device_count, LOCAL)
    mid_branches = [partial(pair_swap, outer_count=N_WIDE * (N_MID // 2), inner_count=N_LOW, qubit=LQ - 3 + place) for place in range(3)]
    vector = lax.switch(swap_qubits[0], mid_branches, vector)
    row_ids = jnp.arange(16, dtype=jnp.int32)[:, None]
    row_bits = jnp.right_shift(row_ids, jnp.arange(4, dtype=jnp.int32)[None, :]) & 1
    row_index = jnp.sum(jnp.left_shift(row_bits, regroup_order[None, :]), axis=1).astype(jnp.int32)
    vector = jnp.take(vector.reshape(2, device_count, 16, LOCAL // 16), row_index, axis=2)
    vector = vector.reshape(2, device_count, LOCAL)
    low_branches = [partial(pair_swap, outer_count=N_WIDE * N_MID * (N_LOW // 2), inner_count=1, qubit=LQ - WQ - 3 + place) for place in range(3)]
    vector = lax.switch(swap_qubits[1], low_branches, vector)
    vector = vector.reshape(2, N_WIDE, N_MID * N_LOW, N_WIDE, LOCAL // N_WIDE)
    vector = jnp.swapaxes(vector, 1, 3).reshape(2, -1)
    for number in range(4, NG):
        vector = apply_gate(vector, gates, number)
    return vector.reshape(state.shape)
```

```python
import jax
import jax.numpy as jnp
from jax import lax
from jax.experimental import pallas as pl
from jax.experimental.pallas import tpu as pltpu
from jax.sharding import PartitionSpec as P

MESH = pl.DeviceIdType.MESH
F32 = jnp.float32
BF16 = jnp.bfloat16
I32 = jnp.int32
NN = (((1,), (0,)), ((), ()))
NT = (((1,), (1,)), ((), ()))
G = 128


def dot(x, w, dims=NN):
    return lax.dot_general(x, w, dims, preferred_element_type=F32)


def split(x):
    high = x.astype(BF16)
    return high, (x - high.astype(F32)).astype(BF16)


def dot3(x, w, dims=NN):
    rows = x[0].shape[0]
    both = dot(jnp.concatenate(x, axis=0), w[0], dims)
    return both[:rows] + both[rows:] + dot(x[0], w[1], dims)


def beside(left, right):
    return jnp.concatenate([left, right], axis=1)


def above(top, bottom):
    return jnp.concatenate([top, bottom], axis=0)


def complex_split(real, imag):
    real_high, real_low = split(real)
    imag_high, imag_low = split(imag)
    return (real_high, imag_high), (real_low, imag_low)


def left_form(pieces):
    return tuple(beside(real, imag) for real, imag in pieces)


def right_form(pieces):
    return tuple(above(beside(real, imag), beside(-imag, real)) for real, imag in pieces)


def row_form(pieces):
    return tuple(above(beside(real, -imag), beside(imag, real)) for real, imag in pieces)


def complex_product(left, right):
    out = dot3(left_form(left), right_form(right))
    return complex_split(out[:, :G], out[:, G:])


def fields_one(index):
    return index >> 6, (index >> 4) & 3, (index >> 3) & 1, index & 7


def fields_two(index):
    return (index >> 3) & 1, (index >> 1) & 3, index & 1, index >> 4


def exchange_lane(first, second, lane, low_bound, high_bound):
    rolled_first = pltpu.roll(first, G // 2, axis=1)
    rolled_second = pltpu.roll(second, G // 2, axis=1)
    return (
        jnp.where(lane < low_bound, first, rolled_second),
        jnp.where(lane >= high_bound, second, rolled_first),
    )


def tiles_two(value):
    shaped = value.reshape(8, 2, 8, G)
    return shaped[:, 0].reshape(64, G), shaped[:, 1].reshape(64, G)


def join_two(first, second):
    shaped = jnp.stack([first.reshape(8, 8, G), second.reshape(8, 8, G)], axis=1)
    return shaped.reshape(G, G)


def kernel(
    state_ref,
    gates_ref,
    low_ref,
    mid_ref,
    top_ref,
    swap_ref,
    order_ref,
    out_ref,
    gate,
    vector,
    keep,
    give,
    gift,
    send_one,
    land_one,
    send_two,
    land_two,
    back_left,
    back_right,
    load_sem,
    gift_send,
    gift_recv,
    send_sem,
    recv_sem,
):
    wide = lax.axis_index("wide")
    mid = lax.axis_index("mid")
    low = lax.axis_index("low")
    depth = wide // 4
    across = lax.rem(wide, 4)
    core = lax.rem(mid, 2)
    place_x = low * 4 + across

    def x_peer(slot):
        return (depth * 4 + lax.rem(slot, 4), mid, slot // 4)

    def z_peer(slot):
        return (slot * 4 + across, mid, low)

    partner = (wide, mid + 1 - 2 * core, low)

    barrier = pltpu.get_barrier_semaphore()
    for step in range(1, 8):
        pl.semaphore_signal(
            barrier, inc=1, device_id=x_peer(lax.rem(place_x + step, 8)), device_id_type=MESH
        )
        pl.semaphore_signal(
            barrier, inc=1, device_id=z_peer(lax.rem(depth + step, 8)), device_id_type=MESH
        )
    pl.semaphore_signal(barrier, inc=1, device_id=partner, device_id_type=MESH)

    first_gates = pltpu.make_async_copy(
        gates_ref.at[pl.ds(0, 4)], gate.at[pl.ds(0, 4)], load_sem.at[0]
    )
    first_gates.start()
    load_state = pltpu.make_async_copy(state_ref, vector, load_sem.at[1])
    load_state.start()
    last_gates = pltpu.make_async_copy(
        gates_ref.at[pl.ds(4, 6)], gate.at[pl.ds(4, 6)], load_sem.at[2]
    )
    last_gates.start()

    first_swap = swap_ref[0]
    second_swap = swap_ref[1]
    low_bound = jnp.where(second_swap == 0, G // 2, G)
    high_bound = jnp.where(second_swap == 0, G // 2, 0)
    lane = lax.broadcasted_iota(I32, (64, G), 1)

    swapped = first_swap + 1
    weights = []
    holds = []
    for place in range(4):
        source = order_ref[place]
        is_swapped = source == swapped
        weights.append(jnp.where(is_swapped, 0, jnp.left_shift(8, source)))
        holds.append(jnp.where(is_swapped, 1, 0))
    low_weight = jnp.where(second_swap == 2, 2, 1)
    spare_weight = 3 - low_weight
    swapped_weight = jnp.left_shift(8, swapped)
    keep_shift = core * swapped_weight
    give_shift = (1 - core) * swapped_weight
    row = lax.broadcasted_iota(I32, (G, G), 0)
    column = lax.broadcasted_iota(I32, (G, G), 1)

    def front_rows(fields):
        low_bit, x_hi, spare, z = fields
        bits = (x_hi >> 1, z & 1, (z >> 1) & 1, z >> 2)
        source = low_bit * low_weight + spare * spare_weight + (x_hi & 1) * 4
        held = jnp.zeros_like(source)
        for bit, weight, hold in zip(bits, weights, holds):
            source = source + bit * weight
            held = held + bit * hold
        return jnp.where(held == core, source, -G)

    def pick(rows, shift):
        return jnp.where(rows + shift == column, 1.0, 0.0).astype(BF16)

    rows_one = front_rows(fields_one(row))
    rows_two = front_rows(fields_two(row))
    picks = jnp.concatenate(
        [
            pick(rows_one, keep_shift),
            pick(rows_two, keep_shift),
            pick(rows_one, give_shift),
            pick(rows_two, give_shift),
        ],
        axis=0,
    )

    low_angle = low_ref[...] + top_ref[0, 0]
    mid_angle = mid_ref[...]
    low_cos, low_sin = jnp.cos(low_angle), jnp.sin(low_angle)
    mid_cos, mid_sin = jnp.cos(mid_angle), jnp.sin(mid_angle)

    def turned(number, cosine, sine):
        real, imag = gate[number, 0], gate[number, 1]
        return complex_split(real * cosine - imag * sine, real * sine + imag * cosine)

    first_gates.wait()
    inner = complex_product(
        turned(2, low_cos, low_sin), complex_split(gate[0, 0], gate[0, 1])
    )
    (three_high, three_low) = complex_split(gate[3, 0], gate[3, 1])
    picked = (
        dot(picks, beside(*three_high)).astype(BF16),
        dot(picks, beside(*three_low)).astype(BF16),
    )
    outer = dot3(picked, right_form(turned(1, mid_cos, mid_sin)))
    real_part, imag_part = outer[:, :G], outer[:, G:]
    outer = jnp.concatenate(
        [
            beside(real_part[:G], -imag_part[:G]),
            beside(imag_part[G : 2 * G], real_part[G : 2 * G]),
            beside(real_part[2 * G : 3 * G], -imag_part[2 * G : 3 * G]),
            beside(imag_part[3 * G :], real_part[3 * G :]),
        ],
        axis=0,
    )
    load_state.wait()
    turned_state = dot3(
        left_form(complex_split(vector[0], vector[1])), row_form(inner), NT
    )
    stacked = above(turned_state[:, :G], turned_state[:, G:])
    front = dot3(split(outer), split(stacked))
    keep[0] = front[:G]
    keep[1] = front[G : 2 * G]
    give[0] = front[2 * G : 3 * G]
    give[1] = front[3 * G :]

    pl.semaphore_wait(barrier, 15)

    gifts = []
    for part in range(2):
        copy = pltpu.make_async_remote_copy(
            src_ref=give.at[part],
            dst_ref=gift.at[part],
            send_sem=gift_send.at[part],
            recv_sem=gift_recv.at[part],
            device_id=partner,
            device_id_type=MESH,
        )
        copy.start()
        gifts.append(copy)

    def block(slot):
        return pl.ds(pl.multiple_of(slot * 16, 16), 16)

    def spread(stage, part, source, target, mine, peer):
        copies = []
        for step in (4, 3, 5, 2, 6, 1, 7):
            slot = lax.rem(mine + step, 8)
            copy = pltpu.make_async_remote_copy(
                src_ref=source.at[part, block(slot), :],
                dst_ref=target.at[part, block(mine), :],
                send_sem=send_sem.at[stage, part, step],
                recv_sem=recv_sem.at[stage, part, step],
                device_id=peer(slot),
                device_id_type=MESH,
            )
            copy.start()
            copies.append(copy)
        target[part, block(mine), :] = source[part, block(mine), :]
        return copies

    gifts[0].wait_recv()
    real_part = keep[0] + gift[0]
    first, second = exchange_lane(real_part[:64], real_part[64:], lane, low_bound, high_bound)
    send_one[0, :64] = first
    send_one[0, 64:] = second
    copies_real = spread(0, 0, send_one, land_one, place_x, x_peer)
    gifts[1].wait_recv()
    imag_part = keep[1] + gift[1]
    first, second = tiles_two(imag_part)
    first, second = exchange_lane(first, second, lane, low_bound, high_bound)
    send_one[1] = join_two(first, second)
    copies_imag = spread(0, 1, send_one, land_one, depth, z_peer)

    last_gates.wait()

    def pieces(number):
        return complex_split(gate[number, 0], gate[number, 1])

    inner = complex_product(pieces(8), complex_product(pieces(6), pieces(4)))
    for level, value in enumerate(row_form(inner)):
        back_right[level] = value

    def natural(fields):
        low_bit, x_hi, spare, z = fields
        return low_bit * low_weight + spare * spare_weight + x_hi * 4 + z * 16

    order = beside(
        jnp.where(natural(fields_two(column)) == row, 1.0, 0.0).astype(BF16),
        jnp.where(natural(fields_one(column)) == row, 1.0, 0.0).astype(BF16),
    )
    outer = complex_product(pieces(9), complex_product(pieces(7), pieces(5)))
    for level, (real, imag) in enumerate(outer):
        real = dot(real, order).astype(BF16)
        imag = dot(imag, order).astype(BF16)
        back_left[level] = above(
            beside(real[:, :G], -imag[:, G:]), beside(imag[:, :G], real[:, G:])
        )

    for copy in copies_real:
        copy.wait_recv()
    for slot in range(8):
        for low_bit in range(2):
            send_two[0, slot * 16 + low_bit * 8 : slot * 16 + low_bit * 8 + 8, :] = land_one[
                0, pl.ds(low_bit * 64 + slot, 8, stride=8), :
            ]
    more_real = spread(1, 0, send_two, land_two, depth, z_peer)
    for copy in copies_imag:
        copy.wait_recv()
    for slot in range(8):
        for spare in range(2):
            start = (slot // 4) * 8 + (slot % 4) * 2 + spare
            send_two[1, slot * 16 + spare * 8 : slot * 16 + spare * 8 + 8, :] = land_one[
                1, pl.ds(start, 8, stride=16), :
            ]
    more_imag = spread(1, 1, send_two, land_two, place_x, x_peer)

    for copy in more_real + more_imag:
        copy.wait_recv()
    first, second = tiles_two(land_two[0])
    first, second = exchange_lane(first, second, lane, low_bound, high_bound)
    real_part = join_two(first, second)
    imag_part = land_two[1]
    first, second = exchange_lane(imag_part[:64], imag_part[64:], lane, low_bound, high_bound)
    stacked = jnp.concatenate([real_part, first, second], axis=0)
    middle = dot3((back_left[0], back_left[1]), split(stacked))
    result = dot3(
        left_form(complex_split(middle[:G], middle[G:])), (back_right[0], back_right[1]), NT
    )
    out_ref[0] = result[:, :G]
    out_ref[1] = result[:, G:]
    for copy in gifts + copies_real + copies_imag + more_real + more_imag:
        copy.wait_send()


def on_device(state, gates, phase_low, phase_mid, phase_top, swap_qubits, regroup_order):
    square = (2, G, G)
    space = pltpu.VMEM
    out = pl.pallas_call(
        kernel,
        out_shape=jax.ShapeDtypeStruct(square, F32),
        in_specs=[
            pl.BlockSpec(memory_space=pl.ANY),
            pl.BlockSpec(memory_space=pl.ANY),
            pl.BlockSpec(memory_space=space),
            pl.BlockSpec(memory_space=space),
            pl.BlockSpec(memory_space=pltpu.SMEM),
            pl.BlockSpec(memory_space=pltpu.SMEM),
            pl.BlockSpec(memory_space=pltpu.SMEM),
        ],
        out_specs=pl.BlockSpec(memory_space=space),
        scratch_shapes=[
            pltpu.VMEM(gates.shape, F32),
            pltpu.VMEM(square, F32),
            pltpu.VMEM(square, F32),
            pltpu.VMEM(square, F32),
            pltpu.VMEM(square, F32),
            pltpu.VMEM(square, F32),
            pltpu.VMEM(square, F32),
            pltpu.VMEM(square, F32),
            pltpu.VMEM(square, F32),
            pltpu.VMEM((2, 2 * G, 2 * G), BF16),
            pltpu.VMEM((2, 2 * G, 2 * G), BF16),
            pltpu.SemaphoreType.DMA((3,)),
            pltpu.SemaphoreType.DMA((2,)),
            pltpu.SemaphoreType.DMA((2,)),
            pltpu.SemaphoreType.DMA((2, 2, 8)),
            pltpu.SemaphoreType.DMA((2, 2, 8)),
        ],
        compiler_params=pltpu.CompilerParams(collective_id=0, has_side_effects=True),
    )(
        state.reshape(square),
        gates,
        phase_low.reshape(1, G),
        phase_mid.reshape(1, G),
        phase_top.reshape(1, 1),
        swap_qubits,
        regroup_order,
    )
    return out.reshape(state.shape)


def solution(mesh):
    return jax.shard_map(
        on_device,
        mesh=mesh,
        in_specs=(
            P(None, "wide", "mid", "low", None),
            P(),
            P(),
            P(),
            P("wide", "mid", "low", None),
            P(),
            P(),
        ),
        out_specs=P(None, "wide", "mid", "low", None),
        check_vma=False,
    )
```

```python
import jax
import jax.numpy as jnp
from jax import lax
from jax.experimental import pallas as pl
from jax.experimental.pallas import tpu as pltpu
from jax.sharding import PartitionSpec as P

MESH = pl.DeviceIdType.MESH
F32 = jnp.float32
BF16 = jnp.bfloat16
I32 = jnp.int32
NN = (((1,), (0,)), ((), ()))
NT = (((1,), (1,)), ((), ()))
G = 128


def dot(x, w, dims=NN):
    return lax.dot_general(x, w, dims, preferred_element_type=F32)


def split(x):
    high = x.astype(BF16)
    return high, (x - high.astype(F32)).astype(BF16)


def dot3(x, w, dims=NN):
    rows = x[0].shape[0]
    both = dot(jnp.concatenate(x, axis=0), w[0], dims)
    return both[:rows] + both[rows:] + dot(x[0], w[1], dims)


def beside(left, right):
    return jnp.concatenate([left, right], axis=1)


def above(top, bottom):
    return jnp.concatenate([top, bottom], axis=0)


def complex_split(real, imag):
    real_high, real_low = split(real)
    imag_high, imag_low = split(imag)
    return (real_high, imag_high), (real_low, imag_low)


def left_form(pieces):
    return tuple(beside(real, imag) for real, imag in pieces)


def right_form(pieces):
    return tuple(above(beside(real, imag), beside(-imag, real)) for real, imag in pieces)


def row_form(pieces):
    return tuple(above(beside(real, -imag), beside(imag, real)) for real, imag in pieces)


def complex_product(left, right):
    out = dot3(left_form(left), right_form(right))
    return complex_split(out[:, :G], out[:, G:])


def fields_one(index):
    return index >> 6, (index >> 4) & 3, (index >> 3) & 1, index & 7


def fields_two(index):
    return (index >> 3) & 1, (index >> 1) & 3, index & 1, index >> 4


def exchange_lane(first, second, lane, low_bound, high_bound):
    rolled_first = pltpu.roll(first, G // 2, axis=1)
    rolled_second = pltpu.roll(second, G // 2, axis=1)
    return (
        jnp.where(lane < low_bound, first, rolled_second),
        jnp.where(lane >= high_bound, second, rolled_first),
    )


def tiles_two(value):
    shaped = value.reshape(8, 2, 8, G)
    return shaped[:, 0].reshape(64, G), shaped[:, 1].reshape(64, G)


def join_two(first, second):
    shaped = jnp.stack([first.reshape(8, 8, G), second.reshape(8, 8, G)], axis=1)
    return shaped.reshape(G, G)


def travel_kernel(
    state_ref,
    gates_ref,
    low_ref,
    mid_ref,
    top_ref,
    swap_hbm,
    order_hbm,
    land_two,
    back_left,
    back_right,
    masks,
    gate,
    vector,
    keep,
    give,
    gift,
    send_one,
    land_one,
    send_two,
    angles,
    top_value,
    swap_ref,
    order_ref,
    load_sem,
    gift_send,
    gift_recv,
    send_sem,
    recv_sem,
):
    wide = lax.axis_index("wide")
    mid = lax.axis_index("mid")
    low = lax.axis_index("low")
    depth = wide // 4
    across = lax.rem(wide, 4)
    core = lax.rem(mid, 2)
    place_x = low * 4 + across

    def x_peer(slot):
        return (depth * 4 + lax.rem(slot, 4), mid, slot // 4)

    def z_peer(slot):
        return (slot * 4 + across, mid, low)

    partner = (wide, mid + 1 - 2 * core, low)

    def load(source, target, number):
        copy = pltpu.make_async_copy(source, target, load_sem.at[number])
        copy.start()
        return copy

    small = [
        load(swap_hbm, swap_ref, 3),
        load(order_hbm, order_ref, 4),
        load(low_ref, angles.at[pl.ds(0, 1)], 5),
        load(mid_ref, angles.at[pl.ds(1, 1)], 6),
        load(top_ref, top_value, 7),
    ]
    first_gates = load(gates_ref.at[pl.ds(0, 4)], gate.at[pl.ds(0, 4)], 0)
    load_state = load(state_ref, vector, 1)
    last_gates = load(gates_ref.at[pl.ds(4, 6)], gate.at[pl.ds(4, 6)], 2)

    barrier = pltpu.get_barrier_semaphore()
    for step in range(1, 8):
        pl.semaphore_signal(
            barrier, inc=1, device_id=x_peer(lax.rem(place_x + step, 8)), device_id_type=MESH
        )
        pl.semaphore_signal(
            barrier, inc=1, device_id=z_peer(lax.rem(depth + step, 8)), device_id_type=MESH
        )
    pl.semaphore_signal(barrier, inc=1, device_id=partner, device_id_type=MESH)

    for copy in small:
        copy.wait()
    first_swap = swap_ref[0]
    second_swap = swap_ref[1]
    low_bound = jnp.where(second_swap == 0, G // 2, G)
    high_bound = jnp.where(second_swap == 0, G // 2, 0)
    lane = lax.broadcasted_iota(I32, (64, G), 1)
    short_lane = lax.broadcasted_iota(I32, (8, G), 1)
    masks[0] = jnp.where(short_lane < low_bound, 1, 0)
    masks[1] = jnp.where(short_lane >= high_bound, 1, 0)

    swapped = first_swap + 1
    weights = []
    holds = []
    for place in range(4):
        source = order_ref[place]
        is_swapped = source == swapped
        weights.append(jnp.where(is_swapped, 0, jnp.left_shift(8, source)))
        holds.append(jnp.where(is_swapped, 1, 0))
    low_weight = jnp.where(second_swap == 2, 2, 1)
    spare_weight = 3 - low_weight
    swapped_weight = jnp.left_shift(8, swapped)
    keep_shift = core * swapped_weight
    give_shift = (1 - core) * swapped_weight
    row = lax.broadcasted_iota(I32, (G, G), 0)
    column = lax.broadcasted_iota(I32, (G, G), 1)

    def front_rows(fields):
        low_bit, x_hi, spare, z = fields
        bits = (x_hi >> 1, z & 1, (z >> 1) & 1, z >> 2)
        source = low_bit * low_weight + spare * spare_weight + (x_hi & 1) * 4
        held = jnp.zeros_like(source)
        for bit, weight, hold in zip(bits, weights, holds):
            source = source + bit * weight
            held = held + bit * hold
        return jnp.where(held == core, source, -G)

    def pick(rows, shift):
        return jnp.where(rows + shift == column, 1.0, 0.0).astype(BF16)

    rows_one = front_rows(fields_one(row))
    rows_two = front_rows(fields_two(row))
    picks = jnp.concatenate(
        [
            pick(rows_one, keep_shift),
            pick(rows_two, keep_shift),
            pick(rows_one, give_shift),
            pick(rows_two, give_shift),
        ],
        axis=0,
    )

    angle = angles[...]
    is_low = lax.broadcasted_iota(I32, (2, G), 0) == 0
    angle = angle + jnp.where(is_low, top_value[0, 0, 0, 0], 0.0)
    cosines, sines = jnp.cos(angle), jnp.sin(angle)
    low_cos, low_sin = cosines[0:1], sines[0:1]
    mid_cos, mid_sin = cosines[1:2], sines[1:2]

    def turned(number, cosine, sine):
        real, imag = gate[number, 0], gate[number, 1]
        return complex_split(real * cosine - imag * sine, real * sine + imag * cosine)

    first_gates.wait()
    inner = complex_product(
        turned(2, low_cos, low_sin), complex_split(gate[0, 0], gate[0, 1])
    )
    (three_high, three_low) = complex_split(gate[3, 0], gate[3, 1])
    picked = (
        dot(picks, beside(*three_high)).astype(BF16),
        dot(picks, beside(*three_low)).astype(BF16),
    )
    picked = tuple(
        jnp.concatenate(
            [
                beside(rows[:G, :G], -rows[:G, G:]),
                beside(rows[G : 2 * G, G:], rows[G : 2 * G, :G]),
                beside(rows[2 * G : 3 * G, :G], -rows[2 * G : 3 * G, G:]),
                beside(rows[3 * G :, G:], rows[3 * G :, :G]),
            ],
            axis=0,
        )
        for rows in picked
    )
    load_state.wait()
    value = dot3(
        row_form(turned(1, mid_cos, mid_sin)), split(above(vector[0], vector[1]))
    )
    value = dot3(left_form(complex_split(value[:G], value[G:])), row_form(inner), NT)
    stacked = above(value[:, :G], value[:, G:])
    front = dot3(picked, split(stacked))
    keep[0] = front[:G]
    keep[1] = front[G : 2 * G]
    give[0] = front[2 * G : 3 * G]
    give[1] = front[3 * G :]

    pl.semaphore_wait(barrier, 15)

    gifts = []
    for part in range(2):
        copy = pltpu.make_async_remote_copy(
            src_ref=give.at[part],
            dst_ref=gift.at[part],
            send_sem=gift_send.at[part],
            recv_sem=gift_recv.at[part],
            device_id=partner,
            device_id_type=MESH,
        )
        copy.start()
        gifts.append(copy)

    def block(slot):
        return pl.ds(pl.multiple_of(slot * 16, 16), 16)

    def spread(stage, part, source, target, mine, peer):
        copies = []
        for step in (4, 3, 5, 2, 6, 1, 7):
            slot = lax.rem(mine + step, 8)
            copy = pltpu.make_async_remote_copy(
                src_ref=source.at[part, block(slot), :],
                dst_ref=target.at[part, block(mine), :],
                send_sem=send_sem.at[stage, part, step],
                recv_sem=recv_sem.at[stage, part, step],
                device_id=peer(slot),
                device_id_type=MESH,
            )
            copy.start()
            copies.append(copy)
        target[part, block(mine), :] = source[part, block(mine), :]
        return copies

    gifts[0].wait_recv()
    real_part = keep[0] + gift[0]
    first, second = exchange_lane(real_part[:64], real_part[64:], lane, low_bound, high_bound)
    send_one[0, :64] = first
    send_one[0, 64:] = second
    copies_real = spread(0, 0, send_one, land_one, place_x, x_peer)
    gifts[1].wait_recv()
    imag_part = keep[1] + gift[1]
    first, second = tiles_two(imag_part)
    first, second = exchange_lane(first, second, lane, low_bound, high_bound)
    send_one[1] = join_two(first, second)
    copies_imag = spread(0, 1, send_one, land_one, depth, z_peer)

    last_gates.wait()

    def pieces(number):
        return complex_split(gate[number, 0], gate[number, 1])

    inner = complex_product(pieces(8), complex_product(pieces(6), pieces(4)))
    for level, value in enumerate(row_form(inner)):
        back_right[level] = value

    def natural(fields):
        low_bit, x_hi, spare, z = fields
        return low_bit * low_weight + spare * spare_weight + x_hi * 4 + z * 16

    order = beside(
        jnp.where(natural(fields_two(column)) == row, 1.0, 0.0).astype(BF16),
        jnp.where(natural(fields_one(column)) == row, 1.0, 0.0).astype(BF16),
    )
    outer = complex_product(pieces(9), complex_product(pieces(7), pieces(5)))
    for level, (real, imag) in enumerate(outer):
        real = dot(real, order).astype(BF16)
        imag = dot(imag, order).astype(BF16)
        back_left[level] = above(
            beside(real[:, :G], -imag[:, G:]), beside(imag[:, :G], real[:, G:])
        )

    for copy in copies_real:
        copy.wait_recv()
    for slot in range(8):
        for low_bit in range(2):
            send_two[0, slot * 16 + low_bit * 8 : slot * 16 + low_bit * 8 + 8, :] = land_one[
                0, pl.ds(low_bit * 64 + slot, 8, stride=8), :
            ]
    more_real = spread(1, 0, send_two, land_two, depth, z_peer)
    for copy in copies_imag:
        copy.wait_recv()
    for slot in range(8):
        for spare in range(2):
            start = (slot // 4) * 8 + (slot % 4) * 2 + spare
            send_two[1, slot * 16 + spare * 8 : slot * 16 + spare * 8 + 8, :] = land_one[
                1, pl.ds(start, 8, stride=16), :
            ]
    more_imag = spread(1, 1, send_two, land_two, place_x, x_peer)

    for copy in more_real + more_imag:
        copy.wait_recv()
    for copy in gifts + copies_real + copies_imag + more_real + more_imag:
        copy.wait_send()


def final_kernel(landed, back_left, back_right, masks, out_ref):
    keep_first = jnp.concatenate([masks[0]] * 8, axis=0) > 0
    keep_second = jnp.concatenate([masks[1]] * 8, axis=0) > 0

    def exchange(first, second):
        rolled_first = pltpu.roll(first, G // 2, axis=1)
        rolled_second = pltpu.roll(second, G // 2, axis=1)
        return (
            jnp.where(keep_first, first, rolled_second),
            jnp.where(keep_second, second, rolled_first),
        )

    real_part = join_two(*exchange(*tiles_two(landed[0])))
    imag_part = landed[1]
    first, second = exchange(imag_part[:64], imag_part[64:])
    stacked = jnp.concatenate([real_part, first, second], axis=0)
    middle = dot3((back_left[0], back_left[1]), split(stacked))
    result = dot3(
        left_form(complex_split(middle[:G], middle[G:])), (back_right[0], back_right[1]), NT
    )
    out_ref[0] = result[:, :G]
    out_ref[1] = result[:, G:]


def on_device(state, gates, phase_low, phase_mid, phase_top, swap_qubits, regroup_order):
    square = (2, G, G)
    doubled = (2, 2 * G, 2 * G)
    vmem = pl.BlockSpec(memory_space=pltpu.VMEM)
    hbm = pl.BlockSpec(memory_space=pltpu.HBM)
    between = pl.pallas_call(
        travel_kernel,
        out_shape=(
            pltpu.VMEM(square, F32),
            pltpu.VMEM(doubled, BF16),
            pltpu.VMEM(doubled, BF16),
            pltpu.VMEM((2, 8, G), I32),
        ),
        in_specs=[hbm] * 7,
        out_specs=(vmem,) * 4,
        scratch_shapes=[
            pltpu.VMEM(gates.shape, F32),
            *[pltpu.VMEM(square, F32)] * 7,
            pltpu.VMEM((2, G), F32),
            pltpu.SMEM((1, 1, 1, 1), F32),
            pltpu.SMEM((2,), I32),
            pltpu.SMEM((4,), I32),
            pltpu.SemaphoreType.DMA((8,)),
            pltpu.SemaphoreType.DMA((2,)),
            pltpu.SemaphoreType.DMA((2,)),
            pltpu.SemaphoreType.DMA((2, 2, 8)),
            pltpu.SemaphoreType.DMA((2, 2, 8)),
        ],
        compiler_params=pltpu.CompilerParams(collective_id=0, has_side_effects=True),
    )(
        state.reshape(square),
        gates,
        phase_low.reshape(1, G),
        phase_mid.reshape(1, G),
        phase_top,
        swap_qubits,
        regroup_order,
    )
    out = pl.pallas_call(
        final_kernel,
        out_shape=jax.ShapeDtypeStruct(square, F32),
        in_specs=[vmem] * 4,
        out_specs=vmem,
        compiler_params=pltpu.CompilerParams(vmem_limit_bytes=8 << 20),
    )(*between)
    return out.reshape(state.shape)


def solution(mesh):
    return jax.shard_map(
        on_device,
        mesh=mesh,
        in_specs=(
            P(None, "wide", "mid", "low", None),
            P(),
            P(),
            P(),
            P("wide", "mid", "low", None),
            P(),
            P(),
        ),
        out_specs=P(None, "wide", "mid", "low", None),
        check_vma=False,
    )
```

```python
import jax
import jax.numpy as jnp
from jax import lax
from jax.experimental import pallas as pl
from jax.experimental.pallas import tpu as pltpu
from jax.sharding import PartitionSpec as P

MESH = pl.DeviceIdType.MESH
F32 = jnp.float32
BF16 = jnp.bfloat16
I32 = jnp.int32
NN = (((1,), (0,)), ((), ()))
NT = (((1,), (1,)), ((), ()))
G = 128


def dot(x, w, dims=NN):
    return lax.dot_general(x, w, dims, preferred_element_type=F32)


def split(x):
    high = x.astype(BF16)
    return high, (x - high.astype(F32)).astype(BF16)


def dot3(x, w, dims=NN):
    rows = x[0].shape[0]
    both = dot(jnp.concatenate(x, axis=0), w[0], dims)
    return both[:rows] + both[rows:] + dot(x[0], w[1], dims)


def beside(left, right):
    return jnp.concatenate([left, right], axis=1)


def above(top, bottom):
    return jnp.concatenate([top, bottom], axis=0)


def complex_split(real, imag):
    real_high, real_low = split(real)
    imag_high, imag_low = split(imag)
    return (real_high, imag_high), (real_low, imag_low)


def left_form(pieces):
    return tuple(beside(real, imag) for real, imag in pieces)


def right_form(pieces):
    return tuple(above(beside(real, imag), beside(-imag, real)) for real, imag in pieces)


def row_form(pieces):
    return tuple(above(beside(real, -imag), beside(imag, real)) for real, imag in pieces)


def complex_product(left, right):
    out = dot3(left_form(left), right_form(right))
    return complex_split(out[:, :G], out[:, G:])


def fields(index):
    return index >> 7, (index >> 5) & 3, (index >> 2) & 7, (index >> 1) & 1, index & 1


def exchange_lane(first, second, lane, low_bound, high_bound):
    rolled_first = pltpu.roll(first, G // 2, axis=1)
    rolled_second = pltpu.roll(second, G // 2, axis=1)
    return (
        jnp.where(lane < low_bound, first, rolled_second),
        jnp.where(lane >= high_bound, second, rolled_first),
    )


def travel_kernel(
    state_ref,
    gates_ref,
    low_ref,
    mid_ref,
    top_ref,
    swap_hbm,
    order_hbm,
    land,
    back_left,
    back_right,
    masks,
    gate,
    vector,
    other,
    send,
    angles,
    turns,
    other_turns,
    top_value,
    swap_ref,
    order_ref,
    load_sem,
    pair_sem,
    row_sem,
    relay_sem,
    gift_send,
    gift_recv,
    send_sem,
    recv_sem,
):
    wide = lax.axis_index("wide")
    mid = lax.axis_index("mid")
    low = lax.axis_index("low")
    depth = wide // 4
    across = lax.rem(wide, 4)
    core = lax.rem(mid, 2)
    place_x = low * 4 + across

    def peer(x, z):
        return (z * 4 + lax.rem(x, 4), mid, x // 4)

    def signal(semaphore, device):
        pl.semaphore_signal(semaphore, inc=1, device_id=device, device_id_type=MESH)

    partner = (wide, mid + 1 - 2 * core, low)

    leads = core == 1
    follows = core == 0
    has_corner = mid < 2
    is_corner = has_corner & (place_x == 0) & (depth == 0)

    barrier = pltpu.get_barrier_semaphore()

    @pl.when(leads)
    def greet_partner():
        signal(barrier, partner)

    def load(source, target, number):
        copy = pltpu.make_async_copy(source, target, load_sem.at[number])
        copy.start()
        return copy

    small = [
        load(swap_hbm, swap_ref, 3),
        load(order_hbm, order_ref, 4),
        load(low_ref, angles.at[pl.ds(0, 1)], 5),
        load(mid_ref, angles.at[pl.ds(1, 1)], 6),
        load(top_ref, top_value, 7),
    ]
    first_gates = load(gates_ref.at[pl.ds(0, 4)], gate.at[pl.ds(0, 4)], 0)
    load_state = load(state_ref, vector, 1)
    last_gates = load(gates_ref.at[pl.ds(4, 6)], gate.at[pl.ds(4, 6)], 2)

    @pl.when(follows)
    def answer_partner():
        pl.semaphore_wait(barrier, 1)
        signal(pair_sem.at[0], partner)

    @pl.when(leads & jnp.logical_not(is_corner))
    def meet_partner():
        pl.semaphore_wait(pair_sem.at[0], 1)

    @pl.when(leads)
    def greet_peers():
        for step in range(1, 8):
            signal(barrier, peer(lax.rem(place_x + step, 8), depth))

        @pl.loop(depth + 1, 8)
        def greet_higher(z):
            for x in range(8):
                signal(barrier, peer(x, z))

    @pl.when(leads & is_corner)
    def meet_late_partner():
        pl.semaphore_wait(pair_sem.at[0], 1)

    def gift(source, target, number):
        copy = pltpu.make_async_remote_copy(
            src_ref=source,
            dst_ref=target,
            send_sem=gift_send.at[number],
            recv_sem=gift_recv.at[number],
            device_id=partner,
            device_id_type=MESH,
        )
        copy.start()
        return copy

    state_gift = gift(state_ref, other, 0)

    for copy in small:
        copy.wait()
    angle = angles[...]
    line = lax.broadcasted_iota(I32, (8, G), 0)
    angle = jnp.where(
        line == 0,
        angle[0:1] + jnp.zeros((8, G), F32),
        jnp.where(line == 1, angle[1:2], top_value[0, 0, 0, 0]),
    )
    turns[0] = jnp.cos(angle)
    turns[1] = jnp.sin(angle)
    turn_gift = gift(turns, other_turns, 1)

    first_swap = swap_ref[0]
    second_swap = swap_ref[1]
    low_bound = jnp.where(second_swap == 0, G // 2, G)
    high_bound = jnp.where(second_swap == 0, G // 2, 0)
    lane = lax.broadcasted_iota(I32, (G, G), 1)
    short_lane = lax.broadcasted_iota(I32, (8, G), 1)
    masks[0] = jnp.where(short_lane < low_bound, 1, 0)
    masks[1] = jnp.where(short_lane >= high_bound, 1, 0)

    swapped = first_swap + 1
    weights = []
    holds = []
    for place in range(4):
        source = order_ref[place]
        is_swapped = source == swapped
        weights.append(jnp.where(is_swapped, 0, jnp.left_shift(8, source)))
        holds.append(jnp.where(is_swapped, 1, 0))
    low_weight = jnp.where(second_swap == 2, 2, 1)
    spare_weight = 3 - low_weight
    core_part = core * jnp.left_shift(8, swapped)
    row = lax.broadcasted_iota(I32, (2 * G, G), 0)
    column = lax.broadcasted_iota(I32, (2 * G, G), 1)
    low_bit, x_hi, z_bits, part, spare = fields(row)
    source = low_bit * low_weight + spare * spare_weight + (x_hi & 1) * 4 + core_part
    held = jnp.zeros_like(source)
    bits = (x_hi >> 1, z_bits & 1, (z_bits >> 1) & 1, z_bits >> 2)
    for bit, weight, hold in zip(bits, weights, holds):
        source = source + bit * weight
        held = held + bit * hold
    picks = jnp.where(source == column, 1.0, 0.0).astype(BF16)
    is_own = held == core
    is_real = part == 0

    low_cos, low_sin = turns[0, 0:1, :], turns[1, 0:1, :]
    mid_cos, mid_sin = turns[0, 1:2, :], turns[1, 1:2, :]

    def turned(real, imag, cosine, sine):
        return complex_split(real * cosine - imag * sine, real * sine + imag * cosine)

    first_gates.wait()
    inner = complex_product(
        turned(gate[2, 0], gate[2, 1], low_cos, low_sin), complex_split(gate[0, 0], gate[0, 1])
    )
    three_high, three_low = complex_split(gate[3, 0], gate[3, 1])
    picked = (
        dot(picks, beside(*three_high)).astype(BF16),
        dot(picks, beside(*three_low)).astype(BF16),
    )
    outer = dot3(picked, right_form(turned(gate[1, 0], gate[1, 1], mid_cos, mid_sin)))
    outer = split(
        beside(
            jnp.where(is_real, outer[:, :G], outer[:, G:]),
            jnp.where(is_real, -outer[:, G:], outer[:, :G]),
        )
    )
    load_state.wait()
    own = left_form(turned(vector[0], vector[1], turns[0, 2:3, :], turns[1, 2:3, :]))

    @pl.when(leads)
    def meet_peers():
        pl.semaphore_wait(barrier, 8 * depth + 7)
        signal(pair_sem.at[0], partner)

        @pl.loop(0, depth)
        def answer_lower(z):
            for x in range(8):
                signal(row_sem.at[depth], peer(x, z))

        @pl.when(is_corner)
        def tell_row():
            for x in range(1, 8):
                signal(row_sem.at[8], peer(x, depth))

    turn_gift.wait_recv()
    state_gift.wait_recv()
    far = left_form(turned(other[0], other[1], other_turns[0, 2:3, :], other_turns[1, 2:3, :]))
    value = dot3(
        tuple(above(mine, theirs) for mine, theirs in zip(own, far)), row_form(inner), NT
    )
    value = above(beside(value[:G, :G], value[G:, :G]), beside(value[:G, G:], value[G:, G:]))
    front = dot3(outer, split(value))
    rows = jnp.where(is_own, front[:, :G], front[:, G:])
    first, second = exchange_lane(rows[:G], rows[G:], lane, low_bound, high_bound)
    send[:G] = first
    send[G:] = second
    mine = place_x * 8 + depth

    def block(slot):
        return pl.ds(pl.multiple_of(slot * 4, 4), 4)

    def travel(x, z):
        slot = x * 8 + z
        return pltpu.make_async_remote_copy(
            src_ref=send.at[block(slot), :],
            dst_ref=land.at[block(mine), :],
            send_sem=send_sem.at[slot],
            recv_sem=recv_sem.at[mine],
            device_id=peer(x, z),
            device_id_type=MESH,
        )

    @pl.when(follows)
    def await_row():
        pl.semaphore_wait(pair_sem.at[0], 1)

    @pl.loop(0, depth + 1)
    def send_lower(z):
        for step in (4, 3, 5, 2, 6, 1, 7, 0):
            x = lax.rem(place_x + step, 8)
            late = has_corner & follows & (x == 0) & (z == 0)

            @pl.when(jnp.logical_not(late | ((z == depth) & (x == place_x))))
            def send_one():
                travel(x, z).start()

    stay = pltpu.make_async_copy(send.at[block(mine), :], land.at[block(mine), :], load_sem.at[0])
    stay.start()

    @pl.loop(depth + 1, 8)
    def send_higher(z):
        @pl.when(leads)
        def relay_higher():
            pl.semaphore_wait(row_sem.at[z], 8)
            signal(relay_sem.at[z], partner)

        @pl.when(follows)
        def await_higher():
            pl.semaphore_wait(relay_sem.at[z], 1)

        for step in (4, 3, 5, 2, 6, 1, 7, 0):
            travel(lax.rem(place_x + step, 8), z).start()

        @pl.when(leads & is_corner)
        def tell_higher():
            for x in range(8):
                signal(row_sem.at[8], peer(x, z))

    last_gates.wait()

    def pieces(number):
        return complex_split(gate[number, 0], gate[number, 1])

    inner = complex_product(pieces(8), complex_product(pieces(6), pieces(4)))
    for level, value in enumerate(row_form(inner)):
        back_right[level] = value

    target = lax.broadcasted_iota(I32, (2 * G, 2 * G), 0)
    low_bit, x_hi, z_bits, part, spare = fields(
        lax.broadcasted_iota(I32, (2 * G, 2 * G), 1)
    )
    source = low_bit * low_weight + spare * spare_weight + x_hi * 4 + z_bits * 16 + part * G
    order = jnp.where(source == target, 1.0, 0.0).astype(BF16)
    outer = complex_product(pieces(9), complex_product(pieces(7), pieces(5)))
    for level, value in enumerate(row_form(outer)):
        back_left[level] = dot(value, order).astype(BF16)

    @pl.when(has_corner & jnp.logical_not(is_corner) & leads)
    def relay_corner():
        pl.semaphore_wait(row_sem.at[8], 1)
        signal(relay_sem.at[8], partner)

    @pl.when(has_corner & jnp.logical_not(is_corner) & follows)
    def send_corner():
        pl.semaphore_wait(relay_sem.at[8], 1)
        travel(0, 0).start()

    stay.wait()

    @pl.loop(1, 64)
    def await_others(step):
        slot = lax.rem(mine + step, 64)
        copy = pltpu.make_async_remote_copy(
            src_ref=send.at[block(slot), :],
            dst_ref=land.at[block(slot), :],
            send_sem=send_sem.at[slot],
            recv_sem=recv_sem.at[slot],
            device_id=peer(slot // 8, lax.rem(slot, 8)),
            device_id_type=MESH,
        )
        copy.wait_send()
        copy.wait_recv()

    state_gift.wait_send()
    turn_gift.wait_send()


def final_kernel(landed, back_left, back_right, masks, out_ref):
    keep_first = jnp.concatenate([masks[0]] * 16, axis=0) > 0
    keep_second = jnp.concatenate([masks[1]] * 16, axis=0) > 0
    first, second = landed[:G], landed[G:]
    rolled_first = pltpu.roll(first, G // 2, axis=1)
    rolled_second = pltpu.roll(second, G // 2, axis=1)
    stacked = above(
        jnp.where(keep_first, first, rolled_second),
        jnp.where(keep_second, second, rolled_first),
    )
    middle = dot3((back_left[0], back_left[1]), split(stacked))
    result = dot3(
        left_form(complex_split(middle[:G], middle[G:])), (back_right[0], back_right[1]), NT
    )
    out_ref[0] = result[:, :G]
    out_ref[1] = result[:, G:]


def on_device(state, gates, phase_low, phase_mid, phase_top, swap_qubits, regroup_order):
    square = (2, G, G)
    doubled = (2, 2 * G, 2 * G)
    vmem = pl.BlockSpec(memory_space=pltpu.VMEM)
    hbm = pl.BlockSpec(memory_space=pltpu.HBM)
    between = pl.pallas_call(
        travel_kernel,
        out_shape=(
            pltpu.VMEM((2 * G, G), F32),
            pltpu.VMEM(doubled, BF16),
            pltpu.VMEM(doubled, BF16),
            pltpu.VMEM((2, 8, G), I32),
        ),
        in_specs=[hbm] * 7,
        out_specs=(vmem,) * 4,
        scratch_shapes=[
            pltpu.VMEM(gates.shape, F32),
            pltpu.VMEM(square, F32),
            pltpu.VMEM(square, F32),
            pltpu.VMEM((2 * G, G), F32),
            pltpu.VMEM((2, G), F32),
            pltpu.VMEM((2, 8, G), F32),
            pltpu.VMEM((2, 8, G), F32),
            pltpu.SMEM((1, 1, 1, 1), F32),
            pltpu.SMEM((2,), I32),
            pltpu.SMEM((4,), I32),
            pltpu.SemaphoreType.DMA((8,)),
            pltpu.SemaphoreType.REGULAR((1,)),
            pltpu.SemaphoreType.REGULAR((9,)),
            pltpu.SemaphoreType.REGULAR((9,)),
            pltpu.SemaphoreType.DMA((2,)),
            pltpu.SemaphoreType.DMA((2,)),
            pltpu.SemaphoreType.DMA((64,)),
            pltpu.SemaphoreType.DMA((64,)),
        ],
        compiler_params=pltpu.CompilerParams(collective_id=0, has_side_effects=True),
    )(
        state.reshape(square),
        gates,
        phase_low.reshape(1, G),
        phase_mid.reshape(1, G),
        phase_top,
        swap_qubits,
        regroup_order,
    )
    out = pl.pallas_call(
        final_kernel,
        out_shape=jax.ShapeDtypeStruct(square, F32),
        in_specs=[vmem] * 4,
        out_specs=vmem,
        compiler_params=pltpu.CompilerParams(vmem_limit_bytes=8 << 20),
    )(*between)
    return out.reshape(state.shape)


def solution(mesh):
    return jax.shard_map(
        on_device,
        mesh=mesh,
        in_specs=(
            P(None, "wide", "mid", "low", None),
            P(),
            P(),
            P(),
            P("wide", "mid", "low", None),
            P(),
            P(),
        ),
        out_specs=P(None, "wide", "mid", "low", None),
        check_vma=False,
    )
```

```python
import jax
import jax.numpy as jnp
from jax import lax
from jax.experimental import pallas as pl
from jax.experimental.pallas import tpu as pltpu
from jax.sharding import PartitionSpec as P

MESH = pl.DeviceIdType.MESH
F32 = jnp.float32
BF16 = jnp.bfloat16
I32 = jnp.int32
NN = (((1,), (0,)), ((), ()))
NT = (((1,), (1,)), ((), ()))
G = 128


def dot(x, w, dims=NN):
    return lax.dot_general(x, w, dims, preferred_element_type=F32)


def split(x):
    high = x.astype(BF16)
    return high, (x - high.astype(F32)).astype(BF16)


def dot3(x, w, dims=NN):
    rows = x[0].shape[0]
    both = dot(jnp.concatenate(x, axis=0), w[0], dims)
    return both[:rows] + both[rows:] + dot(x[0], w[1], dims)


def beside(left, right):
    return jnp.concatenate([left, right], axis=1)


def above(top, bottom):
    return jnp.concatenate([top, bottom], axis=0)


def complex_split(real, imag):
    real_high, real_low = split(real)
    imag_high, imag_low = split(imag)
    return (real_high, imag_high), (real_low, imag_low)


def left_form(pieces):
    return tuple(beside(real, imag) for real, imag in pieces)


def right_form(pieces):
    return tuple(above(beside(real, imag), beside(-imag, real)) for real, imag in pieces)


def row_form(pieces):
    return tuple(above(beside(real, -imag), beside(imag, real)) for real, imag in pieces)


def complex_product(left, right):
    out = dot3(left_form(left), right_form(right))
    return complex_split(out[:, :G], out[:, G:])


def fields(index):
    return index >> 7, (index >> 5) & 3, (index >> 2) & 7, (index >> 1) & 1, index & 1


def exchange_lane(first, second, lane, low_bound, high_bound):
    rolled_first = pltpu.roll(first, G // 2, axis=1)
    rolled_second = pltpu.roll(second, G // 2, axis=1)
    return (
        jnp.where(lane < low_bound, first, rolled_second),
        jnp.where(lane >= high_bound, second, rolled_first),
    )


def travel_kernel(
    state_ref,
    gates_ref,
    low_ref,
    mid_ref,
    top_ref,
    swap_hbm,
    order_hbm,
    land,
    back_left,
    back_right,
    masks,
    gate,
    vector,
    other,
    send,
    angles,
    turns,
    other_turns,
    top_value,
    swap_ref,
    order_ref,
    load_sem,
    pair_sem,
    row_sem,
    relay_sem,
    gift_send,
    gift_recv,
    send_sem,
    recv_sem,
):
    wide = lax.axis_index("wide")
    mid = lax.axis_index("mid")
    low = lax.axis_index("low")
    depth = wide // 4
    across = lax.rem(wide, 4)
    core = lax.rem(mid, 2)
    place_x = low * 4 + across

    def peer(x, z):
        return (z * 4 + lax.rem(x, 4), mid, x // 4)

    def signal(semaphore, device):
        pl.semaphore_signal(semaphore, inc=1, device_id=device, device_id_type=MESH)

    partner = (wide, mid + 1 - 2 * core, low)

    leads = core == 1
    follows = core == 0
    has_corner = mid < 2
    is_corner = has_corner & (place_x == 0) & (depth == 0)

    barrier = pltpu.get_barrier_semaphore()

    @pl.when(leads)
    def greet_partner():
        signal(barrier, partner)

    def load(source, target, number):
        copy = pltpu.make_async_copy(source, target, load_sem.at[number])
        copy.start()
        return copy

    small = [
        load(swap_hbm, swap_ref, 3),
        load(order_hbm, order_ref, 4),
        load(low_ref, angles.at[pl.ds(0, 1)], 5),
        load(mid_ref, angles.at[pl.ds(1, 1)], 6),
        load(top_ref, top_value, 7),
    ]
    first_gates = load(gates_ref.at[pl.ds(0, 4)], gate.at[pl.ds(0, 4)], 0)
    load_state = load(state_ref, vector, 1)
    last_gates = load(gates_ref.at[pl.ds(4, 6)], gate.at[pl.ds(4, 6)], 2)

    @pl.when(follows)
    def answer_partner():
        pl.semaphore_wait(barrier, 1)
        signal(pair_sem.at[0], partner)

    @pl.when(leads & jnp.logical_not(is_corner))
    def meet_partner():
        pl.semaphore_wait(pair_sem.at[0], 1)

    @pl.when(leads)
    def greet_peers():
        for step in range(1, 8):
            signal(barrier, peer(lax.rem(place_x + step, 8), depth))

        @pl.loop(depth + 1, 8)
        def greet_higher(z):
            for x in range(8):
                signal(barrier, peer(x, z))

    @pl.when(leads & is_corner)
    def meet_late_partner():
        pl.semaphore_wait(pair_sem.at[0], 1)

    def gift(source, target, number):
        copy = pltpu.make_async_remote_copy(
            src_ref=source,
            dst_ref=target,
            send_sem=gift_send.at[number],
            recv_sem=gift_recv.at[number],
            device_id=partner,
            device_id_type=MESH,
        )
        copy.start()
        return copy

    state_gift = gift(state_ref, other, 0)

    for copy in small:
        copy.wait()
    angle = angles[...]
    line = lax.broadcasted_iota(I32, (8, G), 0)
    angle = jnp.where(
        line == 0,
        angle[0:1] + jnp.zeros((8, G), F32),
        jnp.where(line == 1, angle[1:2], top_value[0, 0, 0, 0]),
    )
    turns[0] = jnp.cos(angle)
    turns[1] = jnp.sin(angle)
    turn_gift = gift(turns, other_turns, 1)

    first_swap = swap_ref[0]
    second_swap = swap_ref[1]
    low_bound = jnp.where(second_swap == 0, G // 2, G)
    high_bound = jnp.where(second_swap == 0, G // 2, 0)
    lane = lax.broadcasted_iota(I32, (G, G), 1)
    short_lane = lax.broadcasted_iota(I32, (8, G), 1)
    masks[0] = jnp.where(short_lane < low_bound, 1, 0)
    masks[1] = jnp.where(short_lane >= high_bound, 1, 0)

    swapped = first_swap + 1
    weights = []
    holds = []
    for place in range(4):
        source = order_ref[place]
        is_swapped = source == swapped
        weights.append(jnp.where(is_swapped, 0, jnp.left_shift(8, source)))
        holds.append(jnp.where(is_swapped, 1, 0))
    low_weight = jnp.where(second_swap == 2, 2, 1)
    spare_weight = 3 - low_weight
    core_part = core * jnp.left_shift(8, swapped)
    row = lax.broadcasted_iota(I32, (2 * G, G), 0)
    column = lax.broadcasted_iota(I32, (2 * G, G), 1)
    low_bit, x_hi, z_bits, part, spare = fields(row)
    source = low_bit * low_weight + spare * spare_weight + (x_hi & 1) * 4 + core_part
    held = jnp.zeros_like(source)
    bits = (x_hi >> 1, z_bits & 1, (z_bits >> 1) & 1, z_bits >> 2)
    for bit, weight, hold in zip(bits, weights, holds):
        source = source + bit * weight
        held = held + bit * hold
    picks = jnp.where(source == column, 1.0, 0.0).astype(BF16)
    is_own = held == core
    is_real = part == 0

    low_cos, low_sin = turns[0, 0:1, :], turns[1, 0:1, :]
    mid_cos, mid_sin = turns[0, 1:2, :], turns[1, 1:2, :]

    def turned(real, imag, cosine, sine):
        return complex_split(real * cosine - imag * sine, real * sine + imag * cosine)

    first_gates.wait()
    inner = complex_product(
        turned(gate[2, 0], gate[2, 1], low_cos, low_sin), complex_split(gate[0, 0], gate[0, 1])
    )
    three_high, three_low = complex_split(gate[3, 0], gate[3, 1])
    picked = (
        dot(picks, beside(*three_high)).astype(BF16),
        dot(picks, beside(*three_low)).astype(BF16),
    )
    outer = dot3(picked, right_form(turned(gate[1, 0], gate[1, 1], mid_cos, mid_sin)))
    outer = split(
        beside(
            jnp.where(is_real, outer[:, :G], outer[:, G:]),
            jnp.where(is_real, -outer[:, G:], outer[:, :G]),
        )
    )
    load_state.wait()
    own = left_form(turned(vector[0], vector[1], turns[0, 2:3, :], turns[1, 2:3, :]))

    @pl.when(leads)
    def meet_peers():
        pl.semaphore_wait(barrier, 8 * depth + 7)
        signal(pair_sem.at[0], partner)

        @pl.loop(0, depth)
        def answer_lower(z):
            for x in range(8):
                signal(row_sem.at[depth], peer(x, z))

        @pl.when(is_corner)
        def tell_row():
            for x in range(1, 8):
                signal(row_sem.at[8], peer(x, depth))

    turn_gift.wait_recv()
    state_gift.wait_recv()
    far = left_form(turned(other[0], other[1], other_turns[0, 2:3, :], other_turns[1, 2:3, :]))
    value = dot3(
        tuple(above(mine, theirs) for mine, theirs in zip(own, far)), row_form(inner), NT
    )
    value = above(beside(value[:G, :G], value[G:, :G]), beside(value[:G, G:], value[G:, G:]))
    front = dot3(outer, split(value))
    rows = jnp.where(is_own, front[:, :G], front[:, G:])
    first, second = exchange_lane(rows[:G], rows[G:], lane, low_bound, high_bound)
    send[:G] = first
    send[G:] = second
    mine = place_x * 8 + depth

    def block(slot):
        return pl.ds(pl.multiple_of(slot * 4, 4), 4)

    def travel(x, z):
        slot = x * 8 + z
        return pltpu.make_async_remote_copy(
            src_ref=send.at[block(slot), :],
            dst_ref=land.at[block(mine), :],
            send_sem=send_sem,
            recv_sem=recv_sem,
            device_id=peer(x, z),
            device_id_type=MESH,
        )

    @pl.when(follows)
    def await_row():
        pl.semaphore_wait(pair_sem.at[0], 1)

    @pl.loop(0, depth + 1)
    def send_lower(z):
        for step in (4, 3, 5, 2, 6, 1, 7, 0):
            x = lax.rem(place_x + step, 8)
            late = has_corner & follows & (x == 0) & (z == 0)

            @pl.when(jnp.logical_not(late | ((z == depth) & (x == place_x))))
            def send_one():
                travel(x, z).start()

    pltpu.make_async_copy(send.at[block(mine), :], land.at[block(mine), :], recv_sem).start()

    @pl.loop(depth + 1, 8)
    def send_higher(z):
        @pl.when(leads)
        def relay_higher():
            pl.semaphore_wait(row_sem.at[z], 8)
            signal(relay_sem.at[z], partner)

        @pl.when(follows)
        def await_higher():
            pl.semaphore_wait(relay_sem.at[z], 1)

        for step in (4, 3, 5, 2, 6, 1, 7, 0):
            travel(lax.rem(place_x + step, 8), z).start()

        @pl.when(leads & is_corner)
        def tell_higher():
            for x in range(8):
                signal(row_sem.at[8], peer(x, z))

    last_gates.wait()

    def pieces(number):
        return complex_split(gate[number, 0], gate[number, 1])

    inner = complex_product(pieces(8), complex_product(pieces(6), pieces(4)))
    for level, value in enumerate(row_form(inner)):
        back_right[level] = value

    target = lax.broadcasted_iota(I32, (2 * G, 2 * G), 0)
    low_bit, x_hi, z_bits, part, spare = fields(
        lax.broadcasted_iota(I32, (2 * G, 2 * G), 1)
    )
    source = low_bit * low_weight + spare * spare_weight + x_hi * 4 + z_bits * 16 + part * G
    order = jnp.where(source == target, 1.0, 0.0).astype(BF16)
    outer = complex_product(pieces(9), complex_product(pieces(7), pieces(5)))
    for level, value in enumerate(row_form(outer)):
        back_left[level] = dot(value, order).astype(BF16)

    @pl.when(has_corner & jnp.logical_not(is_corner) & leads)
    def relay_corner():
        pl.semaphore_wait(row_sem.at[8], 1)
        signal(relay_sem.at[8], partner)

    @pl.when(has_corner & jnp.logical_not(is_corner) & follows)
    def send_corner():
        pl.semaphore_wait(relay_sem.at[8], 1)
        travel(0, 0).start()

    pltpu.make_async_copy(send, land, recv_sem).wait()
    others = pl.ds(0, 2 * G - 4)
    pltpu.make_async_copy(send.at[others, :], land.at[others, :], send_sem).wait()
    state_gift.wait_send()
    turn_gift.wait_send()


def final_kernel(landed, back_left, back_right, masks, out_ref):
    keep_first = jnp.concatenate([masks[0]] * 16, axis=0) > 0
    keep_second = jnp.concatenate([masks[1]] * 16, axis=0) > 0
    first, second = landed[:G], landed[G:]
    rolled_first = pltpu.roll(first, G // 2, axis=1)
    rolled_second = pltpu.roll(second, G // 2, axis=1)
    stacked = above(
        jnp.where(keep_first, first, rolled_second),
        jnp.where(keep_second, second, rolled_first),
    )
    middle = dot3((back_left[0], back_left[1]), split(stacked))
    result = dot3(
        left_form(complex_split(middle[:G], middle[G:])), (back_right[0], back_right[1]), NT
    )
    out_ref[0] = result[:, :G]
    out_ref[1] = result[:, G:]


def on_device(state, gates, phase_low, phase_mid, phase_top, swap_qubits, regroup_order):
    square = (2, G, G)
    doubled = (2, 2 * G, 2 * G)
    vmem = pl.BlockSpec(memory_space=pltpu.VMEM)
    hbm = pl.BlockSpec(memory_space=pltpu.HBM)
    between = pl.pallas_call(
        travel_kernel,
        out_shape=(
            pltpu.VMEM((2 * G, G), F32),
            pltpu.VMEM(doubled, BF16),
            pltpu.VMEM(doubled, BF16),
            pltpu.VMEM((2, 8, G), I32),
        ),
        in_specs=[hbm] * 7,
        out_specs=(vmem,) * 4,
        scratch_shapes=[
            pltpu.VMEM(gates.shape, F32),
            pltpu.VMEM(square, F32),
            pltpu.VMEM(square, F32),
            pltpu.VMEM((2 * G, G), F32),
            pltpu.VMEM((2, G), F32),
            pltpu.VMEM((2, 8, G), F32),
            pltpu.VMEM((2, 8, G), F32),
            pltpu.SMEM((1, 1, 1, 1), F32),
            pltpu.SMEM((2,), I32),
            pltpu.SMEM((4,), I32),
            pltpu.SemaphoreType.DMA((8,)),
            pltpu.SemaphoreType.REGULAR((1,)),
            pltpu.SemaphoreType.REGULAR((9,)),
            pltpu.SemaphoreType.REGULAR((9,)),
            pltpu.SemaphoreType.DMA((2,)),
            pltpu.SemaphoreType.DMA((2,)),
            pltpu.SemaphoreType.DMA,
            pltpu.SemaphoreType.DMA,
        ],
        compiler_params=pltpu.CompilerParams(collective_id=0, has_side_effects=True),
    )(
        state.reshape(square),
        gates,
        phase_low.reshape(1, G),
        phase_mid.reshape(1, G),
        phase_top,
        swap_qubits,
        regroup_order,
    )
    out = pl.pallas_call(
        final_kernel,
        out_shape=jax.ShapeDtypeStruct(square, F32),
        in_specs=[vmem] * 4,
        out_specs=vmem,
        compiler_params=pltpu.CompilerParams(vmem_limit_bytes=8 << 20),
    )(*between)
    return out.reshape(state.shape)


def solution(mesh):
    return jax.shard_map(
        on_device,
        mesh=mesh,
        in_specs=(
            P(None, "wide", "mid", "low", None),
            P(),
            P(),
            P(),
            P("wide", "mid", "low", None),
            P(),
            P(),
        ),
        out_specs=P(None, "wide", "mid", "low", None),
        check_vma=False,
    )
```
